32 devices in a mesh: section: 4 (over y, x), dp: 4 (over z), mp: 2 (over core).
Axes of the slice: x: 2, y: 2, z: 4, core: 2. Of those that a mesh axis runs over, the one named last changes fastest.
Arguments:
- encoded: float32 [8, 64, 4096], P('dp', None, ('section', 'mp')), may hold values from -6 to 6
- counts: int32 [8], replicated, may hold values from 1 to 64, 384 in all
- owner: int32 [8], replicated, may hold values from 0 to 3, as said below
- w_key: bfloat16 [4, 4096, 2048], P('section', 'dp', 'mp'), may hold values from -0.09375 to 0.09375
- w_value: bfloat16 [4, 4096, 2048], P('section', 'dp', 'mp'), may hold values from -0.09375 to 0.09375
- queries: bfloat16 [4, 16, 128, 2048], P('section', 'dp', None, 'mp'), may hold values from -6 to 6
- grad_out: bfloat16 [4, 16, 128, 2048], P('section', 'dp', None, 'mp'), may hold values from -6 to 6
- dec_mask: int32 [16, 128], P('dp'), may hold values 0 or 1
Outputs:
- attn_out: bfloat16 [4, 16, 128, 2048], P('section', 'dp', None, 'mp')
- d_encoded: float32 [8, 64, 4096], P('dp', None, ('section', 'mp'))
The draws below stay inside these ranges and needn't reach their ends.
Inputs may be any that keep to these rules, and one draw needn't show every extreme that they name: Each owner holds at most 4 dialogues and some owner holds exactly 4.
All inputs are finite; a program needn't handle non-finite values. No bound on the sum of `dec_mask` on one device may be relied on, other than what follows from the above.
Results may differ from the reference program's by a relative error of at most 0.014.
Values may be sent and summed in bfloat16 or wider, within the bound.
A program may use at most 128 MiB of HBM per device.

```python
import math
import jax
import jax.numpy as jnp
import numpy as np
from jax import lax

D = 4096
HEADS = 8
HEAD_DIM = 256
DLG_DEV = 2
CAP = 4
ENC_LEN = 64
DEC_LEN = 128
DIALOGS = 8
SLOTS = 16
N_SECTION = 4
N_DP = 4


def draw_owner(key, part):
    first_key, second_key, third_key = jax.random.split(jax.random.fold_in(key, 11), 3)
    dialog_count = N_DP * DLG_DEV
    hot_owner = jax.random.randint(first_key, (), 0, N_DP).astype(jnp.int32)
    sources = jax.random.permutation(second_key, N_DP).astype(jnp.int32)
    dialog_ids = jnp.arange(dialog_count, dtype=jnp.int32)
    is_hot = (dialog_ids // DLG_DEV == sources[0]) | (dialog_ids == sources[1] * DLG_DEV) | (dialog_ids == sources[2] * DLG_DEV)
    hot_rank = jnp.cumsum(is_hot.astype(jnp.int32)) - 1
    shuffled = jax.random.permutation(third_key, dialog_count).astype(jnp.int32)
    sort_keys = jnp.where(is_hot, hot_rank - dialog_count, shuffled)
    ordering = jnp.argsort(sort_keys, stable=True).astype(jnp.int32)
    offset_rest = dialog_ids - CAP
    pos_owner = jnp.where(dialog_ids < CAP, hot_owner, (hot_owner + 1 + offset_rest % (N_DP - 1)) % N_DP).astype(jnp.int32)
    return jnp.zeros((dialog_count,), jnp.int32).at[ordering].set(pos_owner)


def with_ends(result, rng, least, largest):
    extent = result.shape
    place = [jax.random.randint(jax.random.fold_in(rng, axis), (), 0, extent[axis]) for axis in range(len(extent))]
    result = result.at[tuple(place)].set(least)
    longest = extent.index(max(extent))
    place[longest] = (place[longest] + 1) % extent[longest]
    return result.at[tuple(place)].set(largest)


def shard_levels(key, dims, cuts, low, top_value):
    def one(dim, blocks):
        steps = jax.random.uniform(jax.random.fold_in(jax.random.fold_in(key, 6), dim), (blocks,), jnp.float32, low / len(cuts), top_value / len(cuts))
        return jnp.repeat(jnp.exp(steps), dims[dim] // blocks).reshape((-1,) + (1,) * (len(dims) - dim - 1))

    loudness = one(*cuts[0])
    for cut in cuts[1:]:
        loudness = loudness * one(*cut)
    return loudness


def profile(amount, total, most, lean):
    weights = [(1 << 20) // math.isqrt(standing ** lean) + 1 for standing in range(2, amount + 1)]
    spare, holding = total - most - (amount - 1), [1] * (amount - 1)
    while spare > 0:
        movable = [i for i in range(amount - 1) if holding[i] < most]
        mass, remaining = sum([weights[i] for i in movable]), spare
        for i in movable:
            more = min(most - holding[i], max(1, remaining * weights[i] // mass), spare)
            holding[i] = holding[i] + more
            spare = spare - more
    return np.array([most] + holding)


def ragged(stream_key, number_of, total, limit, lean):
    if number_of == 2:
        one = jax.random.randint(stream_key, (), max(1, total - limit), min(limit, total - 1) + 1)
        return jnp.stack([one, total - one])
    sizes = jnp.asarray(profile(number_of, total, limit, lean), jnp.int32)
    pairs = (number_of - 1) // 2
    giver, receiver = sizes[1:1 + 2 * pairs:2], sizes[2:2 + 2 * pairs:2]
    room = jnp.minimum(giver - 1, limit - receiver)
    passed = jax.random.randint(jax.random.fold_in(stream_key, 1), (pairs,), 0, 1 << 20) % (room + 1)
    sizes = sizes.at[1:1 + 2 * pairs:2].set(giver - passed).at[2:2 + 2 * pairs:2].set(receiver + passed)
    return sizes[jax.random.permutation(jax.random.fold_in(stream_key, 2), number_of)]


def bell_draw(stream_key, shape, width, bound, cuts=(), kind=jnp.bfloat16):
    level = shard_levels(stream_key, shape, cuts, -0.22, 0.18) if cuts else 1.0
    result = jax.random.normal(stream_key, shape, jnp.float32) * width * level
    return jnp.minimum(jnp.maximum(result, -bound), bound).astype(kind)


def setup_inputs(seed: int = 0) -> dict:
    seeds = jax.random.split(jax.random.key(seed), 9)
    return {
        "encoded": bell_draw(seeds[0], (DIALOGS, ENC_LEN, D), 1.0, 6.0, ((0, 4), (2, 8)), jnp.float32),
        "counts": ragged(seeds[1], DIALOGS, DIALOGS * ENC_LEN * 3 // 4, ENC_LEN, 2).astype(jnp.int32),
        "owner": draw_owner(jax.random.fold_in(seeds[8], 71), 0),
        "w_key": bell_draw(seeds[3], (N_SECTION, D, HEADS * HEAD_DIM), D ** -0.5, 0.09375, ((0, 4), (1, 4), (2, 2))),
        "w_value": bell_draw(seeds[4], (N_SECTION, D, HEADS * HEAD_DIM), D ** -0.5, 0.09375, ((0, 4), (1, 4), (2, 2))),
        "queries": bell_draw(seeds[5], (N_SECTION, SLOTS, DEC_LEN, HEADS * HEAD_DIM), 1.0, 6.0, ((0, 4), (1, 4), (3, 2))),
        "grad_out": bell_draw(seeds[6], (N_SECTION, SLOTS, DEC_LEN, HEADS * HEAD_DIM), 1.0, 6.0, ((0, 4), (1, 4), (3, 2))),
        "dec_mask": with_ends((jax.random.randint(seeds[7], (SLOTS, DEC_LEN), 0, 4) < 3).astype(jnp.int32), jax.random.fold_in(seeds[7], 1), 0, 1),
    }


def attend(query_rows, key_rows, value_rows, grad_rows, slot_length, slot_live, answer_mask):
    slot_count, query_len, head_width = query_rows.shape
    key_len = key_rows.shape[1]
    head_count = head_width // HEAD_DIM
    score_scale = HEAD_DIM ** -0.5
    query_heads = query_rows.reshape(slot_count, query_len, head_count, HEAD_DIM).astype(jnp.float32)
    key_heads = key_rows.reshape(slot_count, key_len, head_count, HEAD_DIM).astype(jnp.float32)
    value_heads = value_rows.reshape(slot_count, key_len, head_count, HEAD_DIM).astype(jnp.float32)
    masked_grad = grad_rows * answer_mask.astype(jnp.bfloat16)[:, :, None]
    grad_heads = masked_grad.reshape(slot_count, query_len, head_count, HEAD_DIM).astype(jnp.float32)
    scores = jnp.einsum("cqhd,ckhd->chqk", query_heads, key_heads) * score_scale
    inside = jnp.arange(key_len, dtype=jnp.int32)[None, None, None, :] < slot_length[:, None, None, None]
    unnormed = jnp.where(inside, jnp.exp(scores), 0.0)
    attention = unnormed / (jnp.sum(unnormed, axis=-1, keepdims=True) + (1.0 - slot_live)[:, None, None, None])
    attn_probs = attention.astype(jnp.bfloat16)
    attended = jnp.einsum("chqk,ckhd->cqhd", attn_probs.astype(jnp.float32), value_heads).astype(jnp.bfloat16)
    grad_values = jnp.einsum("chqk,cqhd->ckhd", attn_probs.astype(jnp.float32), grad_heads).astype(jnp.bfloat16)
    grad_probs = jnp.einsum("cqhd,ckhd->chqk", grad_heads, value_heads)
    grad_scores = (attention * (grad_probs - jnp.sum(attention * grad_probs, axis=-1, keepdims=True))).astype(jnp.bfloat16)
    grad_keys = (jnp.einsum("chqk,cqhd->ckhd", grad_scores.astype(jnp.float32), query_heads) * score_scale).astype(jnp.bfloat16)
    return (attended.reshape(slot_count, query_len, head_width),
            grad_keys.reshape(slot_count, key_len, head_width),
            grad_values.reshape(slot_count, key_len, head_width))


def reference(encoded, counts, owner, w_key, w_value, queries, grad_out, dec_mask):
    dialog_ids = jnp.arange(DIALOGS, dtype=jnp.int32)
    is_mine = (owner[None, :] == jnp.arange(N_DP, dtype=jnp.int32)[:, None]).astype(jnp.int32)
    position = jnp.cumsum(is_mine, axis=1) - 1
    picked = is_mine[:, None, :] * (position[:, None, :] == jnp.arange(CAP, dtype=jnp.int32)[None, :, None]).astype(jnp.int32)
    slot_dialog = jnp.sum(picked * dialog_ids[None, None, :], axis=2).reshape(SLOTS).astype(jnp.int32)
    slot_valid = jnp.sum(picked, axis=2).reshape(SLOTS).astype(jnp.int32)
    slot_length = jnp.take(counts, slot_dialog) * slot_valid
    slot_live = slot_valid.astype(jnp.float32)
    slot_keep = slot_valid.astype(jnp.bfloat16)[:, None, None]
    encoded_bf = encoded.astype(jnp.bfloat16).reshape(DIALOGS * ENC_LEN, D)
    head_width = HEADS * HEAD_DIM

    def one_layer(accumulated, pieces):
        key_w, value_w, query_rows, grad_rows = pieces
        key_rows = jnp.dot(encoded_bf, key_w, preferred_element_type=jnp.float32).astype(jnp.bfloat16).reshape(DIALOGS, ENC_LEN, head_width)
        value_rows = jnp.dot(encoded_bf, value_w, preferred_element_type=jnp.float32).astype(jnp.bfloat16).reshape(DIALOGS, ENC_LEN, head_width)
        slot_keys = jnp.take(key_rows, slot_dialog, axis=0) * slot_keep
        slot_values = jnp.take(value_rows, slot_dialog, axis=0) * slot_keep
        attended, grad_keys, grad_values = attend(query_rows, slot_keys, slot_values, grad_rows, slot_length, slot_live, dec_mask)
        dialog_keys = jnp.zeros((DIALOGS, ENC_LEN, head_width), jnp.bfloat16).at[slot_dialog].add(grad_keys * slot_keep)
        dialog_values = jnp.zeros((DIALOGS, ENC_LEN, head_width), jnp.bfloat16).at[slot_dialog].add(grad_values * slot_keep)
        layer_term = jnp.dot(dialog_keys.reshape(-1, head_width), key_w.T, preferred_element_type=jnp.float32)
        layer_term = layer_term + jnp.dot(dialog_values.reshape(-1, head_width), value_w.T, preferred_element_type=jnp.float32)
        return accumulated + layer_term, attended

    start = jnp.zeros((DIALOGS * ENC_LEN, D), jnp.float32)
    accumulated, attn_out = lax.scan(one_layer, start, (w_key, w_value, queries, grad_out))
    return attn_out, accumulated.reshape(DIALOGS, ENC_LEN, D)
```

```python
import functools

import jax
import jax.numpy as jnp
from jax import lax
from jax.experimental import pallas as pl
from jax.experimental.pallas import tpu as pltpu
from jax.sharding import PartitionSpec as P

HEAD_DIM = 256
MESH = pl.DeviceIdType.MESH
F32 = jnp.float32
BF16 = jnp.bfloat16


PIECE_ROWS = 64


def skew(hops):
    return (5 * hops + 1) // 2


def packed_rows(dialogs, key_len):
    return dialogs * key_len * 3 // 4


def lag_of(subs, groups):
    return subs - 1 + skew(groups - 1)


def dot(left, right, left_dim, right_dim):
    return lax.dot_general(
        left, right, (((left_dim,), (right_dim,)), ((), ())), preferred_element_type=F32
    )


def kernel(
    dims,
    counts,
    owner,
    encoded,
    w_key,
    w_value,
    queries,
    grad_out,
    mask,
    attn_out,
    d_encoded,
    table,
    weights,
    q_buf,
    g_buf,
    out_buf,
    enc_cast,
    enc_all,
    enc_pack,
    to_packed,
    from_packed,
    take_slots,
    give_slots,
    delta,
    part,
    recv,
    send,
    own,
    slot_grad,
    acc,
    fin,
    d_send,
    d_pair,
    d_mid,
    d_recv,
    d_fin,
    d_arrived,
    w_sem,
    io_sem,
    out_sem,
    swap_send,
    swap_recv,
    self_sem,
    enc_send_sem,
    enc_pass_sem,
    enc_recv_sem,
    send_sem,
    recv_sem,
    pair_send_sem,
    pair_recv_sem,
    d_send_sem,
    d_recv_sem,
):
    sections, groups, cores = dims
    section = lax.axis_index("section")
    p = lax.axis_index("dp")
    core = lax.axis_index("mp")
    fold = sections // groups
    local_count, key_len, feat = encoded.shape
    dialogs = local_count * groups
    block_rows = local_count * key_len
    cap = queries.shape[0]
    heads = queries.shape[2] // HEAD_DIM
    packed = packed_rows(dialogs, key_len)
    piece_rows = min(PIECE_ROWS, packed)
    subs = packed // piece_rows
    pieces = heads * subs
    lag = lag_of(subs, groups)
    late = skew(groups - 1)
    others = cores - 1
    scale = HEAD_DIM ** (-0.5)

    swap_section, swap_p = p * fold + lax.rem(section, fold), section // fold
    stays = section // fold == p

    def region(s, m):
        rows = pl.multiple_of((s // fold) * block_rows, block_rows)
        cols = pl.multiple_of((lax.rem(s, fold) * cores + m) * feat, feat)
        return pl.ds(rows, block_rows), pl.ds(cols, feat)

    def remote(src, dst, out_sem, in_sem, device):
        return pltpu.make_async_remote_copy(
            src_ref=src,
            dst_ref=dst,
            send_sem=out_sem,
            recv_sem=in_sem,
            device_id=device,
            device_id_type=MESH,
        )

    barrier = pltpu.get_barrier_semaphore()

    def greet(s, z, m):
        pl.semaphore_signal(barrier, inc=1, device_id=(s, z, m), device_id_type=MESH)

    @pl.when(jnp.logical_not(stays))
    def _():
        greet(swap_section, swap_p, core)

    @pl.when(p > 0)
    def _():
        greet(section, p - 1, core)

    @pl.when(p < groups - 1)
    def _():
        greet(section, p + 1, core)

    @pl.loop(1, sections)
    def _(i):
        greet(lax.rem(section + i, sections), p, core)

    for j in range(1, cores):
        greet(section, p, lax.rem(core + j, cores))

    copies = []
    for h in range(heads):
        for kv, ref in enumerate((w_key, w_value)):
            copy = pltpu.make_async_copy(
                ref.at[:, pl.ds(h * HEAD_DIM, HEAD_DIM)],
                weights.at[2 * h + kv],
                w_sem.at[2 * h + kv],
            )
            copy.start()
            copies.append(copy)

    for k, (ref, buf) in enumerate(((queries, q_buf), (grad_out, g_buf))):
        copy = pltpu.make_async_copy(ref, buf, io_sem.at[k])
        copy.start()
        copies.append(copy)

    for a in range(local_count):
        enc_cast[pl.ds(a * key_len, key_len), :] = encoded[a].astype(BF16)

    pl.semaphore_wait(
        barrier,
        sections
        - 1
        + others
        + jnp.where(stays, 0, 1)
        + jnp.where(p > 0, 1, 0)
        + jnp.where(p < groups - 1, 1, 0),
    )

    m_rows, m_cols = region(section, core)
    mine_there = region(swap_section, core)

    def swap_copy():
        return remote(
            enc_cast,
            enc_all.at[mine_there[0], mine_there[1]],
            swap_send.at[0],
            swap_recv.at[0],
            (swap_section, swap_p, core),
        )

    @pl.when(stays)
    def _():
        copy = pltpu.make_async_copy(enc_cast, enc_all.at[m_rows, m_cols], self_sem.at[0])
        copy.start()
        copy.wait()

    @pl.when(jnp.logical_not(stays))
    def _():
        swap_copy().start()

    taken = jnp.int32(0)
    start = jnp.int32(0)
    starts = []
    slot_start = [jnp.int32(0)] * cap
    slot_valid = [jnp.int32(0)] * cap
    slot_length = [jnp.int32(0)] * cap
    for d in range(dialogs):
        mine = (owner[d] == p).astype(jnp.int32)
        for c in range(cap):
            hit = mine * (taken == c).astype(jnp.int32)
            slot_start[c] = slot_start[c] + hit * start
            slot_valid[c] = slot_valid[c] + hit
            slot_length[c] = slot_length[c] + hit * counts[d]
        taken = taken + mine
        starts.append(start)
        start = start + counts[d]
    for c in range(cap):
        table[c] = slot_valid[c]
        table[cap + c] = slot_length[c]

    def one_hot(hit):
        return jnp.where(hit, 1.0, 0.0).astype(BF16)

    def spread_rows(out, firsts, lengths):
        shape = (packed, len(firsts) * key_len)
        at = lax.broadcasted_iota(jnp.int32, (1, shape[1]), 1)
        place = jnp.full((1, shape[1]), -1, jnp.int32)
        for k, (first, length) in enumerate(zip(firsts, lengths)):
            inside = jnp.logical_and(at >= k * key_len, at < k * key_len + length)
            place = jnp.where(inside, at - k * key_len + first, place)
        out[...] = one_hot(lax.broadcasted_iota(jnp.int32, shape, 0) == place)

    def take_rows(out, firsts, lengths):
        shape = (key_len, packed)
        row = lax.broadcasted_iota(jnp.int32, shape, 0)
        col = lax.broadcasted_iota(jnp.int32, shape, 1)
        for k, (first, length) in enumerate(zip(firsts, lengths)):
            hit = jnp.logical_and(col == row + first, row < length)
            out[pl.ds(k * key_len, key_len), :] = one_hot(hit)

    lengths = [counts[d] for d in range(dialogs)]
    spread_rows(to_packed, starts, lengths)
    take_rows(from_packed, starts, lengths)
    take_rows(take_slots, slot_start, slot_length)
    spread_rows(give_slots, slot_start, slot_length)

    for b in range(subs):
        row = lax.broadcasted_iota(jnp.int32, (piece_rows, HEAD_DIM), 0) + b * piece_rows
        ahead_by = jnp.full((piece_rows, HEAD_DIM), groups, jnp.int32)
        for d in range(dialogs):
            ahead_by = jnp.where(row >= starts[d], owner[d] - p, ahead_by)
        delta[b] = ahead_by

    acc[...] = jnp.zeros_like(acc)
    own[...] = jnp.zeros_like(own)

    @pl.when(jnp.logical_not(stays))
    def _():
        remote(
            enc_cast,
            enc_all.at[m_rows, m_cols],
            swap_send.at[0],
            swap_recv.at[0],
            (swap_section, swap_p, core),
        ).wait_recv()

    def block_copy(s, out_sem, device):
        rows, cols = region(s[0], s[1])
        return remote(
            enc_all.at[rows, cols],
            enc_all.at[rows, cols],
            out_sem,
            enc_recv_sem.at[s[0] * cores + s[1]],
            device,
        )

    def spread(i):
        peer = lax.rem(section + i, sections)
        return block_copy((section, core), enc_send_sem.at[peer], (peer, p, core))

    def pass_on(s, j):
        return block_copy(
            (s, core),
            enc_pass_sem.at[s * others + j - 1],
            (section, p, lax.rem(core + j, cores)),
        )

    @pl.loop(1, sections)
    def _(i):
        spread(i).start()

    for j in range(1, cores):
        pass_on(section, j).start()

    for copy in copies:
        copy.wait()

    @pl.loop(1, sections)
    def _(i):
        s = lax.rem(section + sections - i, sections)
        block_copy((s, core), enc_send_sem.at[s], (s, p, core)).wait_recv()
        for j in range(1, cores):
            pass_on(s, j).start()

    @pl.loop(0, sections)
    def _(i):
        s = lax.rem(section + sections - i, sections)
        for j in range(1, cores):
            m = lax.rem(core + j, cores)
            block_copy((s, m), enc_send_sem.at[s], (section, p, m)).wait_recv()

    def hop(way, r):
        return remote(
            send.at[way, r],
            recv.at[way, r],
            send_sem.at[way, r],
            recv_sem.at[way, r],
            (section, p + 1 if way == 0 else p - 1, core),
        )

    def is_first(way):
        return p == 0 if way == 0 else p == groups - 1

    def is_last(way):
        return p == groups - 1 if way == 0 else p == 0

    def far(way):
        return skew(p if way == 0 else groups - 1 - p)

    def within(r, count):
        return jnp.logical_and(r >= 0, r < count)

    def ahead(way, r):
        by = delta[lax.rem(r, subs)]
        return by if way == 0 else -by

    def back_piece(r):
        q = jnp.maximum(r - lag, 0)
        return (q // subs) * subs + lax.rem(r, subs)

    enc_pack[...] = dot(to_packed[...], enc_all[...], 1, 0).astype(BF16)

    def project(h):
        for kv in range(2):
            product = dot(enc_pack[...], weights[2 * h + kv], 1, 0).astype(BF16)
            part[pl.ds(h * subs, subs), kv] = product.reshape(subs, piece_rows, HEAD_DIM)

    def out_copy(h):
        cols = pl.ds(pl.multiple_of(h * HEAD_DIM, HEAD_DIM), HEAD_DIM)
        return pltpu.make_async_copy(out_buf.at[h], attn_out.at[:, :, cols], out_sem.at[h])

    def attend(h):
        cols = pl.ds(pl.multiple_of(h * HEAD_DIM, HEAD_DIM), HEAD_DIM)
        mine = [
            dot(
                take_slots[...],
                part[pl.ds(h * subs, subs), kv].reshape(packed, HEAD_DIM),
                1,
                0,
            ).astype(BF16)
            for kv in range(2)
        ]
        for c in range(cap):
            keep = table[c].astype(F32)
            length = table[cap + c]
            keys = mine[0][c * key_len : (c + 1) * key_len]
            values = mine[1][c * key_len : (c + 1) * key_len]
            q = q_buf[c, :, cols]
            g = g_buf[c, :, cols]
            live = mask[pl.ds(c, 1), :].astype(F32)
            scores = dot(keys, q, 1, 1) * scale
            ok = lax.broadcasted_iota(jnp.int32, scores.shape, 0) < length
            unnormed = jnp.where(ok, jnp.exp(scores), 0.0)
            attention = unnormed / (jnp.sum(unnormed, axis=0, keepdims=True) + (1.0 - keep))
            probs = attention.astype(BF16)
            out_buf[h, c] = dot(probs, values, 0, 0).astype(BF16)
            grad_probs = dot(values, g, 1, 1) * live
            live_probs = (probs.astype(F32) * live).astype(BF16)
            rows = pl.ds(c * key_len, key_len)
            slot_grad[1, rows, :] = dot(live_probs, g, 1, 0).astype(BF16)
            grad_scores = (
                attention
                * (grad_probs - jnp.sum(attention * grad_probs, axis=0, keepdims=True))
            ).astype(BF16)
            slot_grad[0, rows, :] = (dot(grad_scores, q, 1, 0) * scale).astype(BF16)
        for kv in range(2):
            mine_rows = dot(give_slots[...], slot_grad[kv], 1, 0).astype(BF16)
            own[pl.ds(h * subs, subs), kv] = mine_rows.reshape(subs, piece_rows, HEAD_DIM)
        out_copy(h).start()

    rounds = pieces + lag
    steps = rounds + late

    @pl.loop(0, steps)
    def _(t):
        @pl.when(jnp.logical_and(t < pieces, lax.rem(t, subs) == 0))
        def _():
            project(t // subs)

        for way in range(2):
            r = t - far(way)

            @pl.when(within(r, rounds))
            def _(way=way, r=r):
                fwd, bwd = jnp.minimum(r, pieces - 1), back_piece(r)

                @pl.when(jnp.logical_not(is_first(way)))
                def _():
                    hop(way, r).wait_recv()

                @pl.when(jnp.logical_not(jnp.logical_or(is_first(way), is_last(way))))
                def _(fwd=fwd, bwd=bwd):
                    where_to = ahead(way, r)
                    for kv in range(2):
                        came = recv[way, r, kv].astype(F32)
                        send[way, r, kv] = jnp.where(
                            where_to > 0,
                            came + part[fwd, kv].astype(F32),
                            jnp.where(where_to == 0, own[bwd, kv].astype(F32), came),
                        ).astype(BF16)

                    hop(way, r).start()

        whole = t - late

        @pl.when(within(whole, pieces))
        def _():
            @pl.when(p == 0)
            def _():
                part[whole] = (part[whole].astype(F32) + recv[1, whole].astype(F32)).astype(BF16)

            @pl.when(p == groups - 1)
            def _():
                part[whole] = (part[whole].astype(F32) + recv[0, whole].astype(F32)).astype(BF16)

            @pl.when(jnp.logical_and(p > 0, p < groups - 1))
            def _():
                part[whole] = (
                    part[whole].astype(F32)
                    + recv[0, whole].astype(F32)
                    + recv[1, whole].astype(F32)
                ).astype(BF16)

            @pl.when(lax.rem(whole, subs) == subs - 1)
            def _():
                attend(whole // subs)

        for way in range(2):

            @pl.when(jnp.logical_and(is_first(way), t < rounds))
            def _(way=way):
                fwd, bwd = jnp.minimum(t, pieces - 1), back_piece(t)
                where_to = ahead(way, t)
                for kv in range(2):
                    send[way, t, kv] = jnp.where(
                        where_to > 0, part[fwd, kv].astype(F32), own[bwd, kv].astype(F32)
                    ).astype(BF16)
                hop(way, t).start()

        done = t - late - lag

        @pl.when(within(done, pieces))
        def _():
            r = done + lag
            back = back_piece(r)

            def collect(below, above):
                where_to = ahead(0, r)
                for kv in range(2):
                    rows = own[back, kv].astype(F32)
                    if below:
                        rows = jnp.where(where_to < 0, recv[0, r, kv].astype(F32), rows)
                    if above:
                        rows = jnp.where(where_to > 0, recv[1, r, kv].astype(F32), rows)
                    part[back, kv] = rows.astype(BF16)

            @pl.when(p == 0)
            def _():
                collect(False, True)

            @pl.when(p == groups - 1)
            def _():
                collect(True, False)

            @pl.when(jnp.logical_and(p > 0, p < groups - 1))
            def _():
                collect(True, True)

            @pl.when(lax.rem(done, subs) == subs - 1)
            def _():
                h = done // subs
                grads = [
                    part[pl.ds(h * subs, subs), kv].reshape(packed, HEAD_DIM) for kv in range(2)
                ]
                acc[...] += dot(grads[0], weights[2 * h], 1, 1) + dot(
                    grads[1], weights[2 * h + 1], 1, 1
                )

    d_send[...] = dot(from_packed[...], acc[...].astype(BF16), 1, 0).astype(BF16)

    def pair_copy(s, j):
        m = lax.rem(core + j, cores)
        rows, cols = region(s, m)
        k = s * others + j - 1
        return remote(
            d_send.at[rows, cols], d_pair.at[k], pair_send_sem.at[k], pair_recv_sem.at[k],
            (section, p, m),
        )

    def term_copy(s):
        return remote(
            d_mid.at[s], d_recv.at[section], d_send_sem.at[s], d_recv_sem.at[section],
            (s, p, core),
        )

    @pl.loop(1, sections + 1)
    def _(i):
        for j in range(1, cores):
            pair_copy(lax.rem(section + i, sections), j).start()

    def paired(s):
        rows, cols = region(s, core)
        total = d_send[rows, cols].astype(F32)
        for j in range(1, cores):
            pair_copy(s, j).wait_recv()
            total = total + d_pair[s * others + j - 1].astype(F32)
        return total

    @pl.loop(1, sections)
    def _(i):
        s = lax.rem(section + i, sections)
        d_mid[s] = paired(s).astype(BF16)
        term_copy(s).start()

    fin[...] = paired(section)

    @pl.loop(1, sections)
    def _(i):
        s = lax.rem(section + sections - i, sections)
        remote(
            d_mid.at[s], d_recv.at[s], d_send_sem.at[s], d_recv_sem.at[s], (s, p, core)
        ).wait_recv()
        fin[...] += d_recv[s].astype(F32)

    d_fin[...] = fin[...].astype(BF16)

    def back_copy():
        return remote(
            d_fin, d_arrived, swap_send.at[1], swap_recv.at[1], (swap_section, swap_p, core)
        )

    @pl.when(stays)
    def _():
        for a in range(local_count):
            d_encoded[a] = d_fin[pl.ds(a * key_len, key_len), :].astype(F32)

    @pl.when(jnp.logical_not(stays))
    def _():
        back_copy().start()

    for h in range(heads):
        out_copy(h).wait()

    @pl.loop(0, rounds)
    def _(r):
        for way in range(2):

            @pl.when(jnp.logical_not(is_last(way)))
            def _(way=way):
                hop(way, r).wait_send()

    @pl.loop(1, sections)
    def _(i):
        spread(i).wait_send()
        term_copy(lax.rem(section + i, sections)).wait_send()

    @pl.loop(0, sections)
    def _(s):
        for j in range(1, cores):
            pass_on(s, j).wait_send()
            pair_copy(s, j).wait_send()

    @pl.when(jnp.logical_not(stays))
    def _():
        swap_copy().wait_send()
        back_copy().wait()
        for a in range(local_count):
            d_encoded[a] = d_arrived[pl.ds(a * key_len, key_len), :].astype(F32)


def body(dims, encoded, counts, owner, w_key, w_value, queries, grad_out, dec_mask):
    sections, groups, cores = dims
    local_count, key_len, feat = encoded.shape
    dialogs = local_count * groups
    cap, query_len, width = queries.shape[1:]
    model_rows = w_key.shape[1]
    heads = width // HEAD_DIM
    packed = packed_rows(dialogs, key_len)
    piece_rows = min(PIECE_ROWS, packed)
    subs = packed // piece_rows
    pieces = heads * subs
    rounds = pieces + lag_of(subs, groups)
    others = cores - 1
    block_rows = local_count * key_len
    item = (2, piece_rows, HEAD_DIM)
    rows = dialogs * key_len
    dma = pltpu.SemaphoreType.DMA
    vmem = pl.BlockSpec(memory_space=pltpu.VMEM)
    smem = pl.BlockSpec(memory_space=pltpu.SMEM)
    hbm = pl.BlockSpec(memory_space=pl.ANY)
    attended, d_encoded = pl.pallas_call(
        functools.partial(kernel, dims),
        out_shape=(
            jax.ShapeDtypeStruct((cap, query_len, width), BF16),
            jax.ShapeDtypeStruct((local_count, key_len, feat), F32),
        ),
        in_specs=[smem, smem, vmem, hbm, hbm, hbm, hbm, vmem],
        out_specs=(hbm, vmem),
        scratch_shapes=[
            pltpu.SMEM((2 * cap,), jnp.int32),
            pltpu.VMEM((2 * heads, model_rows, HEAD_DIM), BF16),
            pltpu.VMEM((cap, query_len, width), BF16),
            pltpu.VMEM((cap, query_len, width), BF16),
            pltpu.VMEM((heads, cap, query_len, HEAD_DIM), BF16),
            pltpu.VMEM((block_rows, feat), BF16),
            pltpu.VMEM((rows, model_rows), BF16),
            pltpu.VMEM((packed, model_rows), BF16),
            pltpu.VMEM((packed, rows), BF16),
            pltpu.VMEM((rows, packed), BF16),
            pltpu.VMEM((cap * key_len, packed), BF16),
            pltpu.VMEM((packed, cap * key_len), BF16),
            pltpu.VMEM((subs, piece_rows, HEAD_DIM), jnp.int32),
            pltpu.VMEM((pieces,) + item, BF16),
            pltpu.VMEM((2, rounds) + item, BF16),
            pltpu.VMEM((2, rounds) + item, BF16),
            pltpu.VMEM((pieces,) + item, BF16),
            pltpu.VMEM((2, cap * key_len, HEAD_DIM), BF16),
            pltpu.VMEM((packed, model_rows), F32),
            pltpu.VMEM((block_rows, feat), F32),
            pltpu.VMEM((dialogs * key_len, model_rows), BF16),
            pltpu.VMEM((sections * others, block_rows, feat), BF16),
            pltpu.VMEM((sections, block_rows, feat), BF16),
            pltpu.VMEM((sections, block_rows, feat), BF16),
            pltpu.VMEM((block_rows, feat), BF16),
            pltpu.VMEM((block_rows, feat), BF16),
            dma((2 * heads,)),
            dma((2,)),
            dma((heads,)),
            dma((2,)),
            dma((2,)),
            dma((1,)),
            dma((sections,)),
            dma((sections * others,)),
            dma((sections * cores,)),
            dma((2, rounds)),
            dma((2, rounds)),
            dma((sections * others,)),
            dma((sections * others,)),
            dma((sections,)),
            dma((sections,)),
        ],
        compiler_params=pltpu.CompilerParams(
            collective_id=0, has_side_effects=True, vmem_limit_bytes=60 * 1024 * 1024
        ),
    )(counts, owner, encoded, w_key[0], w_value[0], queries[0], grad_out[0], dec_mask)
    return (attended[None], d_encoded)


def solution(mesh):
    placed = (
        P("dp", None, ("section", "mp")),
        P(),
        P(),
        P("section", "dp", "mp"),
        P("section", "dp", "mp"),
        P("section", "dp", None, "mp"),
        P("section", "dp", None, "mp"),
        P("dp", None),
    )
    dims = tuple(mesh.shape[name] for name in ("section", "dp", "mp"))
    return jax.shard_map(
        functools.partial(body, dims),
        mesh=mesh,
        in_specs=placed,
        out_specs=(P("section", "dp", None, "mp"), P("dp", None, ("section", "mp"))),
        check_vma=False,
    )
```

```python
import functools

import jax
import jax.numpy as jnp
from jax import lax
from jax.experimental import pallas as pl
from jax.experimental.pallas import tpu as pltpu
from jax.sharding import PartitionSpec as P

HEAD_DIM = 256
MESH = pl.DeviceIdType.MESH
F32 = jnp.float32
BF16 = jnp.bfloat16


PIECE_ROWS = 128
TOP = 0


def skew(hops):
    return 3 * hops


def packed_rows(dialogs, key_len):
    return dialogs * key_len * 3 // 4


def lag_of(subs, groups):
    return subs - 1 + TOP + skew(groups - 1)


def dot(left, right, left_dim, right_dim):
    return lax.dot_general(
        left, right, (((left_dim,), (right_dim,)), ((), ())), preferred_element_type=F32
    )


def kernel(
    dims,
    counts,
    owner,
    encoded,
    w_key,
    w_value,
    queries,
    grad_out,
    mask,
    attn_out,
    d_encoded,
    table,
    weights,
    q_buf,
    g_buf,
    out_buf,
    enc_cast,
    enc_all,
    enc_pack,
    to_packed,
    from_packed,
    take_slots,
    give_slots,
    delta,
    part,
    recv,
    send,
    own,
    slot_grad,
    held,
    acc,
    d_send,
    d_pair,
    d_mid,
    d_recv,
    d_fin,
    d_cross,
    d_out,
    mid,
    w_sem,
    io_sem,
    out_sem,
    scatter_send,
    scatter_recv,
    along_send,
    along_recv,
    fan_send,
    pass_send,
    block_recv,
    send_sem,
    recv_sem,
    pair_send,
    pair_recv,
    term_send,
    term_recv,
    cross_send,
    cross_recv,
    last_send,
    last_recv,
):
    sections, groups, cores = dims
    section = lax.axis_index("section")
    p = lax.axis_index("dp")
    core = lax.axis_index("mp")
    fold = sections // groups
    local_count, key_len, feat = encoded.shape
    dialogs = local_count * groups
    block_rows = local_count * key_len
    cap = queries.shape[0]
    heads = queries.shape[2] // HEAD_DIM
    packed = packed_rows(dialogs, key_len)
    piece_rows = min(PIECE_ROWS, packed)
    subs = packed // piece_rows
    halves = 2 * heads
    pieces = halves * subs
    lag = lag_of(subs, groups)
    late = skew(groups - 1)
    others = cores - 1
    scale = HEAD_DIM ** (-0.5)

    chunk = block_rows // sections
    spans = [divmod(j * chunk, key_len) for j in range(sections)]

    def remote(src, dst, out_sem, in_sem, device):
        return pltpu.make_async_remote_copy(
            src_ref=src,
            dst_ref=dst,
            send_sem=out_sem,
            recv_sem=in_sem,
            device_id=device,
            device_id_type=MESH,
        )

    barrier = pltpu.get_barrier_semaphore()

    def greet(s, z, m):
        pl.semaphore_signal(barrier, inc=1, device_id=(s, z, m), device_id_type=MESH)

    @pl.loop(1, groups)
    def _(i):
        greet(section, lax.rem(p + i, groups), core)

    @pl.loop(1, sections)
    def _(i):
        greet(lax.rem(section + i, sections), p, core)

    for j in range(1, cores):
        greet(section, p, lax.rem(core + j, cores))

    copies = []
    for h in range(heads):
        for kv, ref in enumerate((w_key, w_value)):
            copy = pltpu.make_async_copy(
                ref.at[:, pl.ds(h * HEAD_DIM, HEAD_DIM)],
                weights.at[2 * h + kv],
                w_sem.at[2 * h + kv],
            )
            copy.start()
            copies.append(copy)

    for k, (ref, buf) in enumerate(((queries, q_buf), (grad_out, g_buf))):
        copy = pltpu.make_async_copy(ref, buf, io_sem.at[k])
        copy.start()
        copies.append(copy)

    for j, (a, first) in enumerate(spans):
        enc_cast[j] = encoded[a, pl.ds(first, chunk), :].astype(BF16)
    mid[section] = enc_cast[section]

    pl.semaphore_wait(barrier, sections - 1 + groups - 1 + others)

    def scatter(s, to):
        return remote(
            enc_cast.at[to], mid.at[s], scatter_send.at[to], scatter_recv.at[s], (to, p, core)
        )

    @pl.loop(1, sections)
    def _(i):
        scatter(section, lax.rem(section + i, sections)).start()

    def near(k):
        return lax.rem(p + k * jnp.where(2 * p < groups, 1, groups - 1), groups)

    def along(z, f, s):
        return remote(
            mid.at[s],
            enc_all.at[f * cores + core, z, section],
            along_send.at[s],
            along_recv.at[z * fold + f],
            (section, s // fold, core),
        )

    @pl.loop(0, sections)
    def _(i):
        s = lax.rem(section + i, sections)

        @pl.when(i > 0)
        def _():
            scatter(s, s).wait_recv()

        @pl.when(s // fold == p)
        def _():
            enc_all[lax.rem(s, fold) * cores + core, p, section] = mid[s]

        @pl.when(s // fold != p)
        def _():
            along(p, lax.rem(s, fold), s).start()

    taken = jnp.int32(0)
    start = jnp.int32(0)
    starts = []
    slot_start = [jnp.int32(0)] * cap
    slot_valid = [jnp.int32(0)] * cap
    slot_length = [jnp.int32(0)] * cap
    for d in range(dialogs):
        mine = (owner[d] == p).astype(jnp.int32)
        for c in range(cap):
            hit = mine * (taken == c).astype(jnp.int32)
            slot_start[c] = slot_start[c] + hit * start
            slot_valid[c] = slot_valid[c] + hit
            slot_length[c] = slot_length[c] + hit * counts[d]
        taken = taken + mine
        starts.append(start)
        start = start + counts[d]
    for c in range(cap):
        table[c] = slot_valid[c]
        table[cap + c] = slot_length[c]

    def one_hot(hit):
        return jnp.where(hit, 1.0, 0.0).astype(BF16)

    def spread_rows(out, firsts, lengths):
        shape = (packed, len(firsts) * key_len)
        at = lax.broadcasted_iota(jnp.int32, (1, shape[1]), 1)
        place = jnp.full((1, shape[1]), -1, jnp.int32)
        for k, (first, length) in enumerate(zip(firsts, lengths)):
            inside = jnp.logical_and(at >= k * key_len, at < k * key_len + length)
            place = jnp.where(inside, at - k * key_len + first, place)
        out[...] = one_hot(lax.broadcasted_iota(jnp.int32, shape, 0) == place)

    def take_rows(out, firsts, lengths):
        shape = (key_len, packed)
        row = lax.broadcasted_iota(jnp.int32, shape, 0)
        col = lax.broadcasted_iota(jnp.int32, shape, 1)
        for k, (first, length) in enumerate(zip(firsts, lengths)):
            hit = jnp.logical_and(col == row + first, row < length)
            out[pl.ds(k * key_len, key_len), :] = one_hot(hit)

    lengths = [counts[d] for d in range(dialogs)]
    spread_rows(to_packed, starts, lengths)
    take_rows(from_packed, starts, lengths)
    take_rows(take_slots, slot_start, slot_length)
    spread_rows(give_slots, slot_start, slot_length)

    for b in range(subs):
        row = lax.broadcasted_iota(jnp.int32, (piece_rows, HEAD_DIM), 0) + b * piece_rows
        ahead_by = jnp.full((piece_rows, HEAD_DIM), groups, jnp.int32)
        for d in range(dialogs):
            ahead_by = jnp.where(row >= starts[d], owner[d] - p, ahead_by)
        delta[b] = ahead_by

    acc[...] = jnp.zeros_like(acc)
    own[...] = jnp.zeros_like(own)

    def block(j, z, f, m, out_sem, device):
        where = enc_all.at[f * cores + m, z, j]
        in_sem = block_recv.at[(j * sections + z * fold + f) * cores + m]
        return remote(where, where, out_sem, in_sem, device)

    def fan(z, f, to):
        out_sem = fan_send.at[to * sections + z * fold + f]
        return block(section, z, f, core, out_sem, (to, p, core))

    def pass_on(j, z, f, i):
        out_sem = pass_send.at[(j * sections + z * fold + f) * others + i - 1]
        return block(j, z, f, core, out_sem, (section, p, lax.rem(core + i, cores)))

    @pl.loop(0, groups + 1)
    def _(k):
        @pl.when(k < groups)
        def _():
            z = near(k)
            for f in range(fold):

                @pl.when(k > 0)
                def _(f=f):
                    along(z, f, z * fold + f).wait_recv()

                @pl.loop(1, sections)
                def _(i, f=f):
                    fan(z, f, lax.rem(section + i, sections)).start()

                for i in range(1, cores):
                    pass_on(section, z, f, i).start()

        @pl.when(k > 0)
        def _():
            z = near(k - 1)

            @pl.loop(1, sections)
            def _(i):
                j = lax.rem(section + sections - i, sections)
                for f in range(fold):
                    block(j, z, f, core, fan_send.at[0], (j, p, core)).wait_recv()
                    for i in range(1, cores):
                        pass_on(j, z, f, i).start()

    for copy in copies:
        copy.wait()

    @pl.loop(0, sections)
    def _(j):
        @pl.loop(0, groups)
        def _(z):
            for f in range(fold):
                for i in range(1, cores):
                    m = lax.rem(core + i, cores)
                    block(j, z, f, m, fan_send.at[0], (section, p, m)).wait_recv()

    def hop(way, r):
        return remote(
            send.at[way, r],
            recv.at[way, r],
            send_sem.at[way, r],
            recv_sem.at[way, r],
            (section, p + 1 if way == 0 else p - 1, core),
        )

    def is_first(way):
        return p == 0 if way == 0 else p == groups - 1

    def is_last(way):
        return p == groups - 1 if way == 0 else p == 0

    def far(way):
        return skew(p if way == 0 else groups - 1 - p)

    def within(r, count):
        return jnp.logical_and(r >= 0, r < count)

    def sides(way, r):
        by = delta[lax.rem(r, subs)]
        return (by > 0 if way == 0 else by < 0), by == 0

    def back_piece(r):
        q = jnp.maximum(r - lag, 0)
        return (q // subs) * subs + lax.rem(r, subs)

    for k in range(fold * cores):
        rows = enc_all[k].reshape(dialogs * key_len, feat)
        enc_pack[:, k * feat : (k + 1) * feat] = dot(to_packed[...], rows, 1, 0).astype(BF16)

    def project(k):
        product = dot(enc_pack[...], weights[k], 1, 0).astype(BF16)
        part[pl.ds(k * subs, subs)] = product.reshape(subs, piece_rows, HEAD_DIM)

    def out_copy(h):
        cols = pl.ds(pl.multiple_of(h * HEAD_DIM, HEAD_DIM), HEAD_DIM)
        return pltpu.make_async_copy(out_buf.at[h], attn_out.at[:, :, cols], out_sem.at[h])

    def half(k):
        return part[pl.ds(k * subs, subs)].reshape(packed, HEAD_DIM)

    def keep_grads(k):
        rows = dot(give_slots[...], slot_grad[...], 1, 0).astype(BF16)
        own[pl.ds(k * subs, subs)] = rows.reshape(subs, piece_rows, HEAD_DIM)

    def attend_keys(h):
        cols = pl.ds(pl.multiple_of(h * HEAD_DIM, HEAD_DIM), HEAD_DIM)
        mine = dot(take_slots[...], half(2 * h), 1, 0).astype(BF16)
        for c in range(cap):
            rows = pl.ds(c * key_len, key_len)
            live = mask[pl.ds(c, 1), :].astype(F32)
            scores = dot(mine[c * key_len : (c + 1) * key_len], q_buf[c, :, cols], 1, 1) * scale
            ok = lax.broadcasted_iota(jnp.int32, scores.shape, 0) < table[cap + c]
            unnormed = jnp.where(ok, jnp.exp(scores), 0.0)
            spare = 1.0 - table[c].astype(F32)
            attention = unnormed / (jnp.sum(unnormed, axis=0, keepdims=True) + spare)
            held[rows, :] = attention
            live_probs = (attention.astype(BF16).astype(F32) * live).astype(BF16)
            slot_grad[rows, :] = dot(live_probs, g_buf[c, :, cols], 1, 0).astype(BF16)
        keep_grads(2 * h)

    def attend_values(h):
        cols = pl.ds(pl.multiple_of(h * HEAD_DIM, HEAD_DIM), HEAD_DIM)
        mine = dot(take_slots[...], half(2 * h + 1), 1, 0).astype(BF16)
        for c in range(cap):
            rows = pl.ds(c * key_len, key_len)
            live = mask[pl.ds(c, 1), :].astype(F32)
            values = mine[c * key_len : (c + 1) * key_len]
            attention = held[rows, :]
            grad_probs = dot(values, g_buf[c, :, cols], 1, 1) * live
            out_buf[h, c] = dot(attention.astype(BF16), values, 0, 0).astype(BF16)
            grad_scores = (
                attention
                * (grad_probs - jnp.sum(attention * grad_probs, axis=0, keepdims=True))
            ).astype(BF16)
            slot_grad[rows, :] = (dot(grad_scores, q_buf[c, :, cols], 1, 0) * scale).astype(BF16)
        keep_grads(2 * h + 1)
        out_copy(h).start()

    rounds = pieces + lag
    steps = rounds + late

    def send_first(t):
        for way in range(2):

            @pl.when(jnp.logical_and(is_first(way), t < rounds))
            def _(way=way):
                forward, _ = sides(way, t)
                send[way, t] = jnp.where(
                    forward,
                    part[jnp.minimum(t, pieces - 1)].astype(F32),
                    own[back_piece(t)].astype(F32),
                ).astype(BF16)
                hop(way, t).start()

    project(0)

    @pl.loop(0, steps)
    def _(t):
        if TOP:
            send_first(t)

        for way in range(2):
            r = t - far(way)

            @pl.when(jnp.logical_and(within(r, rounds), jnp.logical_not(is_first(way))))
            def _(way=way, r=r):
                hop(way, r).wait_recv()

                @pl.when(jnp.logical_not(is_last(way)))
                def _():
                    forward, here = sides(way, r)
                    came = recv[way, r].astype(F32)
                    send[way, r] = jnp.where(
                        forward,
                        came + part[jnp.minimum(r, pieces - 1)].astype(F32),
                        jnp.where(here, own[back_piece(r)].astype(F32), came),
                    ).astype(BF16)
                    hop(way, r).start()

        whole = t - late

        @pl.when(within(whole, pieces))
        def _():
            @pl.when(p == 0)
            def _():
                part[whole] = (part[whole].astype(F32) + recv[1, whole].astype(F32)).astype(BF16)

            @pl.when(p == groups - 1)
            def _():
                part[whole] = (part[whole].astype(F32) + recv[0, whole].astype(F32)).astype(BF16)

            @pl.when(jnp.logical_and(p > 0, p < groups - 1))
            def _():
                part[whole] = (
                    part[whole].astype(F32)
                    + recv[0, whole].astype(F32)
                    + recv[1, whole].astype(F32)
                ).astype(BF16)

            k = whole // subs

            @pl.when(lax.rem(whole, 2 * subs) == subs - 1)
            def _():
                attend_keys(k // 2)

            @pl.when(lax.rem(whole, 2 * subs) == 2 * subs - 1)
            def _():
                attend_values(k // 2)

        if not TOP:
            send_first(t)

        @pl.when(jnp.logical_and(t + 1 < pieces, lax.rem(t + 1, subs) == 0))
        def _():
            project((t + 1) // subs)

        done = t - late - lag

        @pl.when(within(done, pieces))
        def _():
            r = done + lag
            back = back_piece(r)

            def collect(below, above):
                up, here = sides(0, r)
                rows = own[back].astype(F32)
                if below and above:
                    came = jnp.where(up, recv[1, r].astype(F32), recv[0, r].astype(F32))
                else:
                    came = (recv[1, r] if above else recv[0, r]).astype(F32)
                part[back] = jnp.where(here, rows, came).astype(BF16)

            @pl.when(p == 0)
            def _():
                collect(False, True)

            @pl.when(p == groups - 1)
            def _():
                collect(True, False)

            @pl.when(jnp.logical_and(p > 0, p < groups - 1))
            def _():
                collect(True, True)

            @pl.when(lax.rem(done, subs) == subs - 1)
            def _():
                k = done // subs
                acc[...] += dot(half(k), weights[k + 1 - 2 * lax.rem(k, 2)], 1, 1)

    enc_pack[...] = acc[...].astype(BF16)

    def pair_copy(z, f, i):
        m = lax.rem(core + i, cores)
        k = (z * fold + f) * others + i - 1
        return remote(
            d_send.at[f * cores + m, z], d_pair.at[k], pair_send.at[k], pair_recv.at[k],
            (section, p, m),
        )

    def paired(z, f, j):
        total = d_send[f * cores + core, z, j].astype(F32)
        for i in range(1, cores):
            total = total + d_pair[(z * fold + f) * others + i - 1, j].astype(F32)
        return total

    def term_copy(t, s, to):
        return remote(
            d_mid.at[t, to],
            d_recv.at[t, s],
            term_send.at[t * sections + to],
            term_recv.at[t * sections + s],
            (to, p, core),
        )

    @pl.loop(0, groups + 1)
    def _(k):
        @pl.when(k < groups)
        def _():
            z = near(groups - 1 - k)
            rows = pl.ds(pl.multiple_of(z * block_rows, block_rows), block_rows)
            terms = dot(from_packed[rows, :], enc_pack[...], 1, 0).astype(BF16)
            for n in range(fold * cores):
                for j in range(sections):
                    d_send[n, z, j] = terms[
                        j * chunk : (j + 1) * chunk, n * feat : (n + 1) * feat
                    ]
            for f in range(fold):
                for i in range(1, cores):
                    pair_copy(z, f, i).start()

        @pl.when(k > 0)
        def _():
            z = near(groups - k)
            for f in range(fold):
                for i in range(1, cores):
                    pair_copy(z, f, i).wait_recv()

                @pl.loop(1, sections)
                def _(i, f=f):
                    j = lax.rem(section + i, sections)
                    d_mid[z * fold + f, j] = paired(z, f, j).astype(BF16)
                    term_copy(z * fold + f, section, j).start()

    def cross(c, f, z):
        return remote(
            d_fin.at[z * fold + f],
            d_cross.at[c * fold + f],
            cross_send.at[z * fold + f],
            cross_recv.at[c * fold + f],
            (section, z, core),
        )

    @pl.loop(0, groups)
    def _(k):
        z = near(groups - 1 - k)
        for f in range(fold):
            t = z * fold + f
            total = paired(z, f, section)
            for i in range(1, sections):
                s = lax.rem(section + sections - i, sections)
                term_copy(t, s, s).wait_recv()
                total = total + d_recv[t, s].astype(F32)
            d_fin[t] = total.astype(BF16)

            @pl.when(z != p)
            def _(f=f):
                cross(p, f, z).start()

            @pl.when(z == p)
            def _(t=t):
                d_cross[t] = d_fin[t]

    def last(s, to):
        return remote(
            d_cross.at[to], d_out.at[s], last_send.at[to], last_recv.at[s], (to, p, core)
        )

    @pl.loop(0, groups)
    def _(k):
        c = near(groups - 1 - k)
        for f in range(fold):
            s = c * fold + f

            @pl.when(c != p)
            def _(f=f):
                cross(c, f, c).wait_recv()

            @pl.when(s == section)
            def _(s=s):
                d_out[s] = d_cross[s]

            @pl.when(s != section)
            def _(s=s):
                last(section, s).start()

    for j, (a, first) in enumerate(spans):

        @pl.when(section != j)
        def _(j=j):
            last(j, j).wait_recv()

        d_encoded[a, pl.ds(first, chunk), :] = d_out[j].astype(F32)

    for h in range(heads):
        out_copy(h).wait()

    @pl.loop(0, rounds)
    def _(r):
        for way in range(2):

            @pl.when(jnp.logical_not(is_last(way)))
            def _(way=way):
                hop(way, r).wait_send()

    @pl.loop(1, sections)
    def _(i):
        s = lax.rem(section + i, sections)
        scatter(section, s).wait_send()
        last(section, s).wait_send()

    @pl.loop(0, groups)
    def _(z):
        for f in range(fold):
            t = z * fold + f

            @pl.loop(1, sections)
            def _(i, f=f, t=t):
                s = lax.rem(section + i, sections)
                fan(z, f, s).wait_send()
                term_copy(t, section, s).wait_send()

            @pl.loop(0, sections)
            def _(j, f=f):
                for i in range(1, cores):
                    pass_on(j, z, f, i).wait_send()

            for i in range(1, cores):
                pair_copy(z, f, i).wait_send()

            @pl.when(z != p)
            def _(f=f, t=t):
                along(p, f, t).wait_send()
                cross(p, f, z).wait_send()


def body(dims, encoded, counts, owner, w_key, w_value, queries, grad_out, dec_mask):
    sections, groups, cores = dims
    local_count, key_len, feat = encoded.shape
    dialogs = local_count * groups
    cap, query_len, width = queries.shape[1:]
    model_rows = w_key.shape[1]
    heads = width // HEAD_DIM
    packed = packed_rows(dialogs, key_len)
    piece_rows = min(PIECE_ROWS, packed)
    subs = packed // piece_rows
    pieces = 2 * heads * subs
    rounds = pieces + lag_of(subs, groups)
    others = cores - 1
    chunk = local_count * key_len // sections
    tile = (chunk, feat)
    lanes = sections // groups * cores
    item = (piece_rows, HEAD_DIM)
    rows = dialogs * key_len
    dma = pltpu.SemaphoreType.DMA
    vmem = pl.BlockSpec(memory_space=pltpu.VMEM)
    smem = pl.BlockSpec(memory_space=pltpu.SMEM)
    hbm = pl.BlockSpec(memory_space=pl.ANY)
    attended, d_encoded = pl.pallas_call(
        functools.partial(kernel, dims),
        out_shape=(
            jax.ShapeDtypeStruct((cap, query_len, width), BF16),
            jax.ShapeDtypeStruct((local_count, key_len, feat), F32),
        ),
        in_specs=[smem, smem, vmem, hbm, hbm, hbm, hbm, vmem],
        out_specs=(hbm, vmem),
        scratch_shapes=[
            pltpu.SMEM((2 * cap,), jnp.int32),
            pltpu.VMEM((2 * heads, model_rows, HEAD_DIM), BF16),
            pltpu.VMEM((cap, query_len, width), BF16),
            pltpu.VMEM((cap, query_len, width), BF16),
            pltpu.VMEM((heads, cap, query_len, HEAD_DIM), BF16),
            pltpu.VMEM((sections,) + tile, BF16),
            pltpu.VMEM((lanes, groups, sections) + tile, BF16),
            pltpu.VMEM((packed, model_rows), BF16),
            pltpu.VMEM((packed, rows), BF16),
            pltpu.VMEM((rows, packed), BF16),
            pltpu.VMEM((cap * key_len, packed), BF16),
            pltpu.VMEM((packed, cap * key_len), BF16),
            pltpu.VMEM((subs, piece_rows, HEAD_DIM), jnp.int32),
            pltpu.VMEM((pieces,) + item, BF16),
            pltpu.VMEM((2, rounds) + item, BF16),
            pltpu.VMEM((2, rounds) + item, BF16),
            pltpu.VMEM((pieces,) + item, BF16),
            pltpu.VMEM((cap * key_len, HEAD_DIM), BF16),
            pltpu.VMEM((cap * key_len, query_len), F32),
            pltpu.VMEM((packed, model_rows), F32),
            pltpu.VMEM((lanes, groups, sections) + tile, BF16),
            pltpu.VMEM((sections * others, sections) + tile, BF16),
            pltpu.VMEM((sections, sections) + tile, BF16),
            pltpu.VMEM((sections, sections) + tile, BF16),
            pltpu.VMEM((sections,) + tile, BF16),
            pltpu.VMEM((sections,) + tile, BF16),
            pltpu.VMEM((sections,) + tile, BF16),
            pltpu.VMEM((sections,) + tile, BF16),
            dma((2 * heads,)),
            dma((2,)),
            dma((heads,)),
            dma((sections,)),
            dma((sections,)),
            dma((sections,)),
            dma((sections,)),
            dma((sections * sections,)),
            dma((sections * sections * others,)),
            dma((sections * sections * cores,)),
            dma((2, rounds)),
            dma((2, rounds)),
            dma((sections * others,)),
            dma((sections * others,)),
            dma((sections * sections,)),
            dma((sections * sections,)),
            dma((sections,)),
            dma((sections,)),
            dma((sections,)),
            dma((sections,)),
        ],
        compiler_params=pltpu.CompilerParams(
            collective_id=0, has_side_effects=True, vmem_limit_bytes=60 * 1024 * 1024
        ),
    )(counts, owner, encoded, w_key[0], w_value[0], queries[0], grad_out[0], dec_mask)
    return (attended[None], d_encoded)


def solution(mesh):
    placed = (
        P("dp", None, ("section", "mp")),
        P(),
        P(),
        P("section", "dp", "mp"),
        P("section", "dp", "mp"),
        P("section", "dp", None, "mp"),
        P("section", "dp", None, "mp"),
        P("dp", None),
    )
    dims = tuple(mesh.shape[name] for name in ("section", "dp", "mp"))
    return jax.shard_map(
        functools.partial(body, dims),
        mesh=mesh,
        in_specs=placed,
        out_specs=(P("section", "dp", None, "mp"), P("dp", None, ("section", "mp"))),
        check_vma=False,
    )
```

```python
import functools

import jax
import jax.numpy as jnp
from jax import lax
from jax.experimental import pallas as pl
from jax.experimental.pallas import tpu as pltpu
from jax.sharding import PartitionSpec as P

HEAD_DIM = 256
MESH = pl.DeviceIdType.MESH
F32 = jnp.float32
BF16 = jnp.bfloat16


PIECE_ROWS = 128
TOP = 0


def skew(hops):
    return 3 * hops


def packed_rows(dialogs, key_len):
    return dialogs * key_len * 3 // 4


def lag_of(subs, groups):
    return subs - 1 + TOP + skew(groups - 1)


def dot(left, right, left_dim, right_dim):
    return lax.dot_general(
        left, right, (((left_dim,), (right_dim,)), ((), ())), preferred_element_type=F32
    )


def kernel(
    dims,
    counts,
    owner,
    encoded,
    w_key,
    w_value,
    queries,
    grad_out,
    mask,
    out_buf,
    d_out,
    table,
    weights,
    q_buf,
    g_buf,
    enc_cast,
    enc_all,
    enc_pack,
    to_packed,
    from_packed,
    take_slots,
    give_slots,
    delta,
    part,
    recv,
    send,
    own,
    slot_grad,
    held,
    acc,
    d_send,
    d_pair,
    d_mid,
    d_recv,
    d_fin,
    d_cross,
    mid,
    w_sem,
    io_sem,
    scatter_send,
    scatter_recv,
    along_send,
    along_recv,
    fan_send,
    pass_send,
    block_recv,
    send_sem,
    recv_sem,
    pair_send,
    pair_recv,
    term_send,
    term_recv,
    cross_send,
    cross_recv,
    last_send,
    last_recv,
):
    sections, groups, cores = dims
    section = lax.axis_index("section")
    p = lax.axis_index("dp")
    core = lax.axis_index("mp")
    fold = sections // groups
    local_count, key_len, feat = encoded.shape
    dialogs = local_count * groups
    block_rows = local_count * key_len
    cap = queries.shape[0]
    heads = queries.shape[2] // HEAD_DIM
    packed = packed_rows(dialogs, key_len)
    piece_rows = min(PIECE_ROWS, packed)
    subs = packed // piece_rows
    halves = 2 * heads
    pieces = halves * subs
    lag = lag_of(subs, groups)
    late = skew(groups - 1)
    others = cores - 1
    scale = HEAD_DIM ** (-0.5)

    chunk = block_rows // sections
    spans = [divmod(j * chunk, key_len) for j in range(sections)]

    def remote(src, dst, out_sem, in_sem, device):
        return pltpu.make_async_remote_copy(
            src_ref=src,
            dst_ref=dst,
            send_sem=out_sem,
            recv_sem=in_sem,
            device_id=device,
            device_id_type=MESH,
        )

    barrier = pltpu.get_barrier_semaphore()

    def greet(s, z, m):
        pl.semaphore_signal(barrier, inc=1, device_id=(s, z, m), device_id_type=MESH)

    @pl.loop(1, groups)
    def _(i):
        greet(section, lax.rem(p + i, groups), core)

    @pl.loop(1, sections)
    def _(i):
        greet(lax.rem(section + i, sections), p, core)

    for j in range(1, cores):
        greet(section, p, lax.rem(core + j, cores))

    copies = []
    for h in range(heads):
        for kv, ref in enumerate((w_key, w_value)):
            copy = pltpu.make_async_copy(
                ref.at[:, pl.ds(h * HEAD_DIM, HEAD_DIM)],
                weights.at[2 * h + kv],
                w_sem.at[2 * h + kv],
            )
            copy.start()
            copies.append(copy)

    for k, (ref, buf) in enumerate(((queries, q_buf), (grad_out, g_buf))):
        copy = pltpu.make_async_copy(ref, buf, io_sem.at[k])
        copy.start()
        copies.append(copy)

    for j, (a, first) in enumerate(spans):
        enc_cast[j] = encoded[a, pl.ds(first, chunk), :].astype(BF16)
    mid[section] = enc_cast[section]

    pl.semaphore_wait(barrier, sections - 1 + groups - 1 + others)

    def scatter(s, to):
        return remote(
            enc_cast.at[to], mid.at[s], scatter_send.at[to], scatter_recv.at[s], (to, p, core)
        )

    @pl.loop(1, sections)
    def _(i):
        scatter(section, lax.rem(section + i, sections)).start()

    def near(k):
        return lax.rem(p + k * jnp.where(2 * p < groups, 1, groups - 1), groups)

    def along(z, f, s):
        return remote(
            mid.at[s],
            enc_all.at[f * cores + core, z, section],
            along_send.at[s],
            along_recv.at[z * fold + f],
            (section, s // fold, core),
        )

    @pl.loop(0, sections)
    def _(i):
        s = lax.rem(section + i, sections)

        @pl.when(i > 0)
        def _():
            scatter(s, s).wait_recv()

        @pl.when(s // fold == p)
        def _():
            enc_all[lax.rem(s, fold) * cores + core, p, section] = mid[s]

        @pl.when(s // fold != p)
        def _():
            along(p, lax.rem(s, fold), s).start()

    taken = jnp.int32(0)
    start = jnp.int32(0)
    starts = []
    slot_start = [jnp.int32(0)] * cap
    slot_valid = [jnp.int32(0)] * cap
    slot_length = [jnp.int32(0)] * cap
    for d in range(dialogs):
        mine = (owner[d] == p).astype(jnp.int32)
        for c in range(cap):
            hit = mine * (taken == c).astype(jnp.int32)
            slot_start[c] = slot_start[c] + hit * start
            slot_valid[c] = slot_valid[c] + hit
            slot_length[c] = slot_length[c] + hit * counts[d]
        taken = taken + mine
        starts.append(start)
        start = start + counts[d]
    for c in range(cap):
        table[c] = slot_valid[c]
        table[cap + c] = slot_length[c]

    def one_hot(hit):
        return jnp.where(hit, 1.0, 0.0).astype(BF16)

    def spread_rows(out, firsts, lengths):
        shape = (packed, len(firsts) * key_len)
        at = lax.broadcasted_iota(jnp.int32, (1, shape[1]), 1)
        place = jnp.full((1, shape[1]), -1, jnp.int32)
        for k, (first, length) in enumerate(zip(firsts, lengths)):
            inside = jnp.logical_and(at >= k * key_len, at < k * key_len + length)
            place = jnp.where(inside, at - k * key_len + first, place)
        out[...] = one_hot(lax.broadcasted_iota(jnp.int32, shape, 0) == place)

    def take_rows(out, firsts, lengths):
        shape = (key_len, packed)
        row = lax.broadcasted_iota(jnp.int32, shape, 0)
        col = lax.broadcasted_iota(jnp.int32, shape, 1)
        for k, (first, length) in enumerate(zip(firsts, lengths)):
            hit = jnp.logical_and(col == row + first, row < length)
            out[pl.ds(k * key_len, key_len), :] = one_hot(hit)

    lengths = [counts[d] for d in range(dialogs)]
    spread_rows(to_packed, starts, lengths)
    take_rows(from_packed, starts, lengths)
    take_rows(take_slots, slot_start, slot_length)
    spread_rows(give_slots, slot_start, slot_length)

    for b in range(subs):
        row = lax.broadcasted_iota(jnp.int32, (piece_rows, HEAD_DIM), 0) + b * piece_rows
        ahead_by = jnp.full((piece_rows, HEAD_DIM), groups, jnp.int32)
        for d in range(dialogs):
            ahead_by = jnp.where(row >= starts[d], owner[d] - p, ahead_by)
        delta[b] = ahead_by

    acc[...] = jnp.zeros_like(acc)
    own[...] = jnp.zeros_like(own)

    def block(j, z, f, m, out_sem, device):
        where = enc_all.at[f * cores + m, z, j]
        in_sem = block_recv.at[(j * sections + z * fold + f) * cores + m]
        return remote(where, where, out_sem, in_sem, device)

    def fan(z, f, to):
        out_sem = fan_send.at[to * sections + z * fold + f]
        return block(section, z, f, core, out_sem, (to, p, core))

    def pass_on(j, z, f, i):
        out_sem = pass_send.at[(j * sections + z * fold + f) * others + i - 1]
        return block(j, z, f, core, out_sem, (section, p, lax.rem(core + i, cores)))

    @pl.loop(0, groups + 1)
    def _(k):
        @pl.when(k < groups)
        def _():
            z = near(k)
            for f in range(fold):

                @pl.when(k > 0)
                def _(f=f):
                    along(z, f, z * fold + f).wait_recv()

                @pl.loop(1, sections)
                def _(i, f=f):
                    fan(z, f, lax.rem(section + i, sections)).start()

                for i in range(1, cores):
                    pass_on(section, z, f, i).start()

        @pl.when(k > 0)
        def _():
            z = near(k - 1)

            @pl.loop(1, sections)
            def _(i):
                j = lax.rem(section + sections - i, sections)
                for f in range(fold):
                    block(j, z, f, core, fan_send.at[0], (j, p, core)).wait_recv()
                    for i in range(1, cores):
                        pass_on(j, z, f, i).start()

    for copy in copies:
        copy.wait()

    @pl.loop(0, sections)
    def _(j):
        @pl.loop(0, groups)
        def _(z):
            for f in range(fold):
                for i in range(1, cores):
                    m = lax.rem(core + i, cores)
                    block(j, z, f, m, fan_send.at[0], (section, p, m)).wait_recv()

    def hop(way, r):
        return remote(
            send.at[way, r],
            recv.at[way, r],
            send_sem.at[way, r],
            recv_sem.at[way, r],
            (section, p + 1 if way == 0 else p - 1, core),
        )

    def is_first(way):
        return p == 0 if way == 0 else p == groups - 1

    def is_last(way):
        return p == groups - 1 if way == 0 else p == 0

    def far(way):
        return skew(p if way == 0 else groups - 1 - p)

    def within(r, count):
        return jnp.logical_and(r >= 0, r < count)

    def sides(way, r):
        by = delta[lax.rem(r, subs)]
        return (by > 0 if way == 0 else by < 0), by == 0

    def back_piece(r):
        q = jnp.maximum(r - lag, 0)
        return (q // subs) * subs + lax.rem(r, subs)

    for k in range(fold * cores):
        rows = enc_all[k].reshape(dialogs * key_len, feat)
        enc_pack[:, k * feat : (k + 1) * feat] = dot(to_packed[...], rows, 1, 0).astype(BF16)

    def project(k):
        product = dot(enc_pack[...], weights[k], 1, 0).astype(BF16)
        part[pl.ds(k * subs, subs)] = product.reshape(subs, piece_rows, HEAD_DIM)

    def half(k):
        return part[pl.ds(k * subs, subs)].reshape(packed, HEAD_DIM)

    def keep_grads(k):
        rows = dot(give_slots[...], slot_grad[...], 1, 0).astype(BF16)
        own[pl.ds(k * subs, subs)] = rows.reshape(subs, piece_rows, HEAD_DIM)

    def attend_keys(h):
        cols = pl.ds(pl.multiple_of(h * HEAD_DIM, HEAD_DIM), HEAD_DIM)
        mine = dot(take_slots[...], half(2 * h), 1, 0).astype(BF16)
        for c in range(cap):
            rows = pl.ds(c * key_len, key_len)
            live = mask[pl.ds(c, 1), :].astype(F32)
            scores = dot(mine[c * key_len : (c + 1) * key_len], q_buf[c, :, cols], 1, 1) * scale
            ok = lax.broadcasted_iota(jnp.int32, scores.shape, 0) < table[cap + c]
            unnormed = jnp.where(ok, jnp.exp(scores), 0.0)
            spare = 1.0 - table[c].astype(F32)
            attention = unnormed / (jnp.sum(unnormed, axis=0, keepdims=True) + spare)
            held[rows, :] = attention
            live_probs = (attention.astype(BF16).astype(F32) * live).astype(BF16)
            slot_grad[rows, :] = dot(live_probs, g_buf[c, :, cols], 1, 0).astype(BF16)
        keep_grads(2 * h)

    def attend_values(h):
        cols = pl.ds(pl.multiple_of(h * HEAD_DIM, HEAD_DIM), HEAD_DIM)
        mine = dot(take_slots[...], half(2 * h + 1), 1, 0).astype(BF16)
        for c in range(cap):
            rows = pl.ds(c * key_len, key_len)
            live = mask[pl.ds(c, 1), :].astype(F32)
            values = mine[c * key_len : (c + 1) * key_len]
            attention = held[rows, :]
            grad_probs = dot(values, g_buf[c, :, cols], 1, 1) * live
            out_buf[h, c] = dot(attention.astype(BF16), values, 0, 0).astype(BF16)
            grad_scores = (
                attention
                * (grad_probs - jnp.sum(attention * grad_probs, axis=0, keepdims=True))
            ).astype(BF16)
            slot_grad[rows, :] = (dot(grad_scores, q_buf[c, :, cols], 1, 0) * scale).astype(BF16)
        keep_grads(2 * h + 1)

    rounds = pieces + lag
    steps = rounds + late

    def send_first(t):
        for way in range(2):

            @pl.when(jnp.logical_and(is_first(way), t < rounds))
            def _(way=way):
                forward, _ = sides(way, t)
                send[way, t] = jnp.where(
                    forward,
                    part[jnp.minimum(t, pieces - 1)].astype(F32),
                    own[back_piece(t)].astype(F32),
                ).astype(BF16)
                hop(way, t).start()

    project(0)

    @pl.loop(0, steps)
    def _(t):
        if TOP:
            send_first(t)

        for way in range(2):
            r = t - far(way)

            @pl.when(jnp.logical_and(within(r, rounds), jnp.logical_not(is_first(way))))
            def _(way=way, r=r):
                hop(way, r).wait_recv()

                @pl.when(jnp.logical_not(is_last(way)))
                def _():
                    forward, here = sides(way, r)
                    came = recv[way, r].astype(F32)
                    send[way, r] = jnp.where(
                        forward,
                        came + part[jnp.minimum(r, pieces - 1)].astype(F32),
                        jnp.where(here, own[back_piece(r)].astype(F32), came),
                    ).astype(BF16)
                    hop(way, r).start()

        whole = t - late

        @pl.when(within(whole, pieces))
        def _():
            @pl.when(p == 0)
            def _():
                part[whole] = (part[whole].astype(F32) + recv[1, whole].astype(F32)).astype(BF16)

            @pl.when(p == groups - 1)
            def _():
                part[whole] = (part[whole].astype(F32) + recv[0, whole].astype(F32)).astype(BF16)

            @pl.when(jnp.logical_and(p > 0, p < groups - 1))
            def _():
                part[whole] = (
                    part[whole].astype(F32)
                    + recv[0, whole].astype(F32)
                    + recv[1, whole].astype(F32)
                ).astype(BF16)

            k = whole // subs

            @pl.when(lax.rem(whole, 2 * subs) == subs - 1)
            def _():
                attend_keys(k // 2)

            @pl.when(lax.rem(whole, 2 * subs) == 2 * subs - 1)
            def _():
                attend_values(k // 2)

        if not TOP:
            send_first(t)

        @pl.when(jnp.logical_and(t + 1 < pieces, lax.rem(t + 1, subs) == 0))
        def _():
            project((t + 1) // subs)

        done = t - late - lag

        @pl.when(within(done, pieces))
        def _():
            r = done + lag
            back = back_piece(r)

            def collect(below, above):
                up, here = sides(0, r)
                rows = own[back].astype(F32)
                if below and above:
                    came = jnp.where(up, recv[1, r].astype(F32), recv[0, r].astype(F32))
                else:
                    came = (recv[1, r] if above else recv[0, r]).astype(F32)
                part[back] = jnp.where(here, rows, came).astype(BF16)

            @pl.when(p == 0)
            def _():
                collect(False, True)

            @pl.when(p == groups - 1)
            def _():
                collect(True, False)

            @pl.when(jnp.logical_and(p > 0, p < groups - 1))
            def _():
                collect(True, True)

            @pl.when(lax.rem(done, subs) == subs - 1)
            def _():
                k = done // subs
                acc[...] += dot(half(k), weights[k + 1 - 2 * lax.rem(k, 2)], 1, 1)

    enc_pack[...] = acc[...].astype(BF16)

    def pair_copy(z, f, i):
        m = lax.rem(core + i, cores)
        k = (z * fold + f) * others + i - 1
        return remote(
            d_send.at[f * cores + m, z], d_pair.at[k], pair_send.at[k], pair_recv.at[k],
            (section, p, m),
        )

    def paired(z, f, j):
        total = d_send[f * cores + core, z, j].astype(F32)
        for i in range(1, cores):
            total = total + d_pair[(z * fold + f) * others + i - 1, j].astype(F32)
        return total

    def term_copy(t, s, to):
        return remote(
            d_mid.at[t, to],
            d_recv.at[t, s],
            term_send.at[t * sections + to],
            term_recv.at[t * sections + s],
            (to, p, core),
        )

    @pl.loop(0, groups + 1)
    def _(k):
        @pl.when(k < groups)
        def _():
            z = near(groups - 1 - k)
            rows = pl.ds(pl.multiple_of(z * block_rows, block_rows), block_rows)
            terms = dot(from_packed[rows, :], enc_pack[...], 1, 0).astype(BF16)
            for n in range(fold * cores):
                for j in range(sections):
                    d_send[n, z, j] = terms[
                        j * chunk : (j + 1) * chunk, n * feat : (n + 1) * feat
                    ]
            for f in range(fold):
                for i in range(1, cores):
                    pair_copy(z, f, i).start()

        @pl.when(k > 0)
        def _():
            z = near(groups - k)
            for f in range(fold):
                for i in range(1, cores):
                    pair_copy(z, f, i).wait_recv()

                @pl.loop(1, sections)
                def _(i, f=f):
                    j = lax.rem(section + i, sections)
                    d_mid[z * fold + f, j] = paired(z, f, j).astype(BF16)
                    term_copy(z * fold + f, section, j).start()

    def cross(c, f, z):
        return remote(
            d_fin.at[z * fold + f],
            d_cross.at[c * fold + f],
            cross_send.at[z * fold + f],
            cross_recv.at[c * fold + f],
            (section, z, core),
        )

    @pl.loop(0, groups)
    def _(k):
        z = near(groups - 1 - k)
        for f in range(fold):
            t = z * fold + f
            total = paired(z, f, section)
            for i in range(1, sections):
                s = lax.rem(section + sections - i, sections)
                term_copy(t, s, s).wait_recv()
                total = total + d_recv[t, s].astype(F32)
            d_fin[t] = total.astype(BF16)

            @pl.when(z != p)
            def _(f=f):
                cross(p, f, z).start()

            @pl.when(z == p)
            def _(t=t):
                d_cross[t] = d_fin[t]

    def last(s, to):
        return remote(
            d_cross.at[to], d_out.at[s], last_send.at[to], last_recv.at[s], (to, p, core)
        )

    @pl.loop(0, groups)
    def _(k):
        c = near(groups - 1 - k)
        for f in range(fold):
            s = c * fold + f

            @pl.when(c != p)
            def _(f=f):
                cross(c, f, c).wait_recv()

            @pl.when(s == section)
            def _(s=s):
                d_out[s] = d_cross[s]

            @pl.when(s != section)
            def _(s=s):
                last(section, s).start()

    @pl.loop(1, sections)
    def _(i):
        j = lax.rem(section + i, sections)
        last(j, j).wait_recv()

    @pl.loop(0, rounds)
    def _(r):
        for way in range(2):

            @pl.when(jnp.logical_not(is_last(way)))
            def _(way=way):
                hop(way, r).wait_send()

    @pl.loop(1, sections)
    def _(i):
        s = lax.rem(section + i, sections)
        scatter(section, s).wait_send()
        last(section, s).wait_send()

    @pl.loop(0, groups)
    def _(z):
        for f in range(fold):
            t = z * fold + f

            @pl.loop(1, sections)
            def _(i, f=f, t=t):
                s = lax.rem(section + i, sections)
                fan(z, f, s).wait_send()
                term_copy(t, section, s).wait_send()

            @pl.loop(0, sections)
            def _(j, f=f):
                for i in range(1, cores):
                    pass_on(j, z, f, i).wait_send()

            for i in range(1, cores):
                pair_copy(z, f, i).wait_send()

            @pl.when(z != p)
            def _(f=f, t=t):
                along(p, f, t).wait_send()
                cross(p, f, z).wait_send()


def finish(out_buf, d_out, attn_out, d_encoded, sem):
    heads, chunk, key_len = out_buf.shape[0], d_out.shape[1], d_encoded.shape[1]
    copies = []
    for h in range(heads):
        cols = pl.ds(h * HEAD_DIM, HEAD_DIM)
        copy = pltpu.make_async_copy(out_buf.at[h], attn_out.at[:, :, cols], sem.at[h])
        copy.start()
        copies.append(copy)
    for j in range(d_out.shape[0]):
        a, first = divmod(j * chunk, key_len)
        d_encoded[a, pl.ds(first, chunk), :] = d_out[j].astype(F32)
    for copy in copies:
        copy.wait()


def body(dims, encoded, counts, owner, w_key, w_value, queries, grad_out, dec_mask):
    sections, groups, cores = dims
    local_count, key_len, feat = encoded.shape
    dialogs = local_count * groups
    cap, query_len, width = queries.shape[1:]
    model_rows = w_key.shape[1]
    heads = width // HEAD_DIM
    packed = packed_rows(dialogs, key_len)
    piece_rows = min(PIECE_ROWS, packed)
    subs = packed // piece_rows
    pieces = 2 * heads * subs
    rounds = pieces + lag_of(subs, groups)
    others = cores - 1
    chunk = local_count * key_len // sections
    tile = (chunk, feat)
    lanes = sections // groups * cores
    item = (piece_rows, HEAD_DIM)
    rows = dialogs * key_len
    dma = pltpu.SemaphoreType.DMA
    vmem = pl.BlockSpec(memory_space=pltpu.VMEM)
    smem = pl.BlockSpec(memory_space=pltpu.SMEM)
    hbm = pl.BlockSpec(memory_space=pl.ANY)
    attended, gathered = pl.pallas_call(
        functools.partial(kernel, dims),
        out_shape=(
            pltpu.VMEM((heads, cap, query_len, HEAD_DIM), BF16),
            pltpu.VMEM((sections,) + tile, BF16),
        ),
        in_specs=[smem, smem, vmem, hbm, hbm, hbm, hbm, vmem],
        out_specs=(vmem, vmem),
        scratch_shapes=[
            pltpu.SMEM((2 * cap,), jnp.int32),
            pltpu.VMEM((2 * heads, model_rows, HEAD_DIM), BF16),
            pltpu.VMEM((cap, query_len, width), BF16),
            pltpu.VMEM((cap, query_len, width), BF16),
            pltpu.VMEM((sections,) + tile, BF16),
            pltpu.VMEM((lanes, groups, sections) + tile, BF16),
            pltpu.VMEM((packed, model_rows), BF16),
            pltpu.VMEM((packed, rows), BF16),
            pltpu.VMEM((rows, packed), BF16),
            pltpu.VMEM((cap * key_len, packed), BF16),
            pltpu.VMEM((packed, cap * key_len), BF16),
            pltpu.VMEM((subs, piece_rows, HEAD_DIM), jnp.int32),
            pltpu.VMEM((pieces,) + item, BF16),
            pltpu.VMEM((2, rounds) + item, BF16),
            pltpu.VMEM((2, rounds) + item, BF16),
            pltpu.VMEM((pieces,) + item, BF16),
            pltpu.VMEM((cap * key_len, HEAD_DIM), BF16),
            pltpu.VMEM((cap * key_len, query_len), F32),
            pltpu.VMEM((packed, model_rows), F32),
            pltpu.VMEM((lanes, groups, sections) + tile, BF16),
            pltpu.VMEM((sections * others, sections) + tile, BF16),
            pltpu.VMEM((sections, sections) + tile, BF16),
            pltpu.VMEM((sections, sections) + tile, BF16),
            pltpu.VMEM((sections,) + tile, BF16),
            pltpu.VMEM((sections,) + tile, BF16),
            pltpu.VMEM((sections,) + tile, BF16),
            dma((2 * heads,)),
            dma((2,)),
            dma((sections,)),
            dma((sections,)),
            dma((sections,)),
            dma((sections,)),
            dma((sections * sections,)),
            dma((sections * sections * others,)),
            dma((sections * sections * cores,)),
            dma((2, rounds)),
            dma((2, rounds)),
            dma((sections * others,)),
            dma((sections * others,)),
            dma((sections * sections,)),
            dma((sections * sections,)),
            dma((sections,)),
            dma((sections,)),
            dma((sections,)),
            dma((sections,)),
        ],
        compiler_params=pltpu.CompilerParams(
            collective_id=0, has_side_effects=True, vmem_limit_bytes=60 * 1024 * 1024
        ),
    )(counts, owner, encoded, w_key[0], w_value[0], queries[0], grad_out[0], dec_mask)
    attn_out, d_encoded = pl.pallas_call(
        finish,
        out_shape=(
            jax.ShapeDtypeStruct((cap, query_len, width), BF16),
            jax.ShapeDtypeStruct((local_count, key_len, feat), F32),
        ),
        in_specs=[vmem, vmem],
        out_specs=(hbm, vmem),
        scratch_shapes=[dma((heads,))],
    )(*(pltpu.with_memory_space_constraint(x, pltpu.VMEM) for x in (attended, gathered)))
    return (attn_out[None], d_encoded)


def solution(mesh):
    placed = (
        P("dp", None, ("section", "mp")),
        P(),
        P(),
        P("section", "dp", "mp"),
        P("section", "dp", "mp"),
        P("section", "dp", None, "mp"),
        P("section", "dp", None, "mp"),
        P("dp", None),
    )
    dims = tuple(mesh.shape[name] for name in ("section", "dp", "mp"))
    return jax.shard_map(
        functools.partial(body, dims),
        mesh=mesh,
        in_specs=placed,
        out_specs=(P("section", "dp", None, "mp"), P("dp", None, ("section", "mp"))),
        check_vma=False,
    )
```
